32 devices in a mesh: dp: 8 (over z, y), mp: 4 (over x, core).
Axes of the slice: x: 2, y: 2, z: 4, core: 2. Of those that a mesh axis runs over, the one named last changes fastest.
Arguments:
- tokens: bfloat16 [2, 4096, 768], P(None, 'dp'), may hold values from -6 to 6
- cotangent: bfloat16 [2, 4096, 768], P(None, 'dp'), may hold values from -6 to 6
- qkv_weight: bfloat16 [768, 3, 768], P('dp', None, 'mp'), may hold values from -0.21875 to 0.21875
- head_bias: bfloat16 [2, 4, 192], P(None, 'mp', 'dp'), may hold values from -3 to 3
- out_weight: bfloat16 [768, 768], P('mp', 'dp'), may hold values from -0.875 to 0.875
- up_weight: bfloat16 [768, 3072], P('dp', 'mp'), may hold values from -0.21875 to 0.21875
- up_bias: bfloat16 [4, 768], P('mp', 'dp'), may hold values from -3 to 3
- down_weight: bfloat16 [3072, 768], P('mp', 'dp'), may hold values from -0.109375 to 0.109375
- mem_qk: bfloat16 [2, 768, 768], P(None, 'dp'), may hold values from -0.21875 to 0.21875
- mem_value: bfloat16 [768, 768], P('dp'), may hold values from -0.875 to 0.875
- norm_gain: bfloat16 [2, 768], P(None, 'dp'), may hold values from 0.5 to 1.5
- shift_bias: bfloat16 [4, 768], P(None, 'dp'), may hold values from -2 to 2
- parents: int32 [2, 8], replicated, may hold values from -1 to 6, as said below
Outputs:
- mixed: bfloat16 [2, 4096, 768], P(None, ('dp', 'mp'))
- tokens_grad: bfloat16 [2, 4096, 768], P(None, 'dp')
- qkv_grad: float32 [768, 3, 768], P('dp', None, 'mp')
- head_bias_grad: float32 [2, 4, 192], P(None, 'mp', 'dp')
- out_grad: float32 [768, 768], P('mp', 'dp')
- up_grad: float32 [768, 3072], P('dp', 'mp')
- up_bias_grad: float32 [4, 768], P('mp', 'dp')
- down_grad: float32 [3072, 768], P('mp', 'dp')
- mem_qk_grad: float32 [2, 768, 768], P(None, 'dp')
- mem_value_grad: float32 [768, 768], P('dp')
- norm_gain_grad: float32 [2, 768], P(None, 'dp')
- shift_bias_grad: float32 [4, 768], P(None, 'dp')
The draws below stay inside these ranges and needn't reach their ends.
Inputs may be any that keep to these rules, and one draw needn't show every extreme that they name: parents[b, n] is the parent segment of segment n in micro-batch b: -1 for the first segment of each aligned group of 8 segments, else an earlier segment of the same group; the last segment of each group has the segment before it as parent.
All inputs are finite; a program needn't handle non-finite values.
Results may differ from the reference program's by a relative error of at most 0.015.
Values may be sent and summed in bfloat16 or wider, within the bound.
A program may use at most 256 MiB of HBM per device.

```python
import jax
import jax.numpy as jnp
from jax import lax

D = 768
FF = 3072
HEADS = 12
HEAD_DIM = 64
MEM = 16
SEG = 512
TREE = 8
MICRO = 2
SEGS = 8
TOKENS = 4096
N_MP = 4


def draw_parents(key, part):
    position = jnp.arange(SEGS, dtype=jnp.int32) % TREE
    slot_index = jnp.arange(SEGS, dtype=jnp.int32)
    backward = jax.random.randint(key, (MICRO, SEGS), 0, 3).astype(jnp.int32)
    backward = jnp.minimum(backward, jnp.maximum(position - 1, 0))
    backward = jnp.where(position == TREE - 1, 0, backward)
    parent = slot_index - 1 - backward
    return jnp.where(position == 0, -1, parent).astype(jnp.int32)


def block_scale(key, extent, pieces, low, high):
    def one(axis_at, shards_of):
        heights = jax.random.uniform(jax.random.fold_in(jax.random.fold_in(key, 6), axis_at), (shards_of,), jnp.float32, low / len(pieces), high / len(pieces))
        return jnp.repeat(jnp.exp(heights), extent[axis_at] // shards_of).reshape((-1,) + (1,) * (len(extent) - axis_at - 1))

    gain = one(*pieces[0])
    for cut in pieces[1:]:
        gain = gain * one(*cut)
    return gain


def bell_draw(key, extent, scale, bound, split=(), kind=jnp.bfloat16):
    values = jax.random.normal(key, extent, jnp.float32) * scale
    if len(split) > 0:
        values = block_scale(key, extent, split, -0.22, 0.18) * values
    return jnp.clip(values, min=-bound, max=bound).astype(kind)


def setup_inputs(seed: int = 0) -> dict:
    streams_of = jax.random.split(jax.random.key(seed), 14)
    tokens = bell_draw(streams_of[0], (MICRO, TOKENS, D), 1.0, 6.0, ((1, 8),))
    cotangent = bell_draw(streams_of[1], (MICRO, TOKENS, D), 1.0, 6.0, ((1, 8),))
    qkv_weight = bell_draw(streams_of[2], (D, 3, D), D ** -0.5, 0.21875, ((0, 8), (2, 4)))
    head_bias = bell_draw(streams_of[3], (2, N_MP, D // N_MP), 0.5, 3.0, ((1, 4), (2, 8)))
    out_weight = bell_draw(streams_of[4], (D, D), (D // 16) ** -0.5, 0.875, ((0, 4), (1, 8)))
    up_weight = bell_draw(streams_of[5], (D, FF), D ** -0.5, 0.21875, ((0, 8), (1, 4)))
    up_bias = bell_draw(streams_of[6], (N_MP, FF // N_MP), 0.5, 3.0, ((0, 4), (1, 8)))
    down_weight = bell_draw(streams_of[7], (FF, D), FF ** -0.5, 0.109375, ((0, 4), (1, 8)))
    mem_qk = bell_draw(streams_of[8], (2, D, D), D ** -0.5, 0.21875, ((1, 8),))
    mem_value = bell_draw(streams_of[9], (D, D), (D // 16) ** -0.5, 0.875, ((0, 8),))
    norm_gain = jnp.clip(1.0 + 0.1 * jax.random.normal(streams_of[10], (2, D), jnp.float32), 0.5, 1.5).astype(jnp.bfloat16)
    shift_bias = bell_draw(streams_of[11], (4, D), 0.3, 2.0, ((1, 8),))
    parents = draw_parents(jax.random.fold_in(streams_of[13], 71), 0)
    return {"tokens": tokens, "cotangent": cotangent, "qkv_weight": qkv_weight, "head_bias": head_bias, "out_weight": out_weight, "up_weight": up_weight, "up_bias": up_bias, "down_weight": down_weight, "mem_qk": mem_qk, "mem_value": mem_value, "norm_gain": norm_gain, "shift_bias": shift_bias, "parents": parents}


@jax.custom_vjp
def low(v):
    return lax.optimization_barrier(v.astype(jnp.bfloat16)).astype(jnp.float32)

@jax.custom_vjp
def low_back(v):
    return v

def low_keep(v):
    return (low(v), None)

def low_pass(kept, grad):
    return (grad,)

def back_keep(v):
    return (v, None)

def back_low(kept, grad):
    return (low(grad),)
low.defvjp(low_keep, low_pass)
low_back.defvjp(back_keep, back_low)
EPSILON = 1e-05
HIGHEST = lax.Precision.HIGHEST

def layer_norm(values, gains, offset):
    center = values - lax.optimization_barrier(jnp.mean(values, -1, keepdims=True))
    spread = lax.optimization_barrier(jnp.mean(center * center, -1, keepdims=True))
    return center * lax.rsqrt(spread + EPSILON) * gains + offset

def gelu_tanh(values):
    return jax.nn.gelu(values, approximate=True)

def dpfp_features(values):
    rectified = jnp.concatenate([jax.nn.relu(values), jax.nn.relu(-values)], -1)
    return jnp.concatenate([rectified * jnp.roll(rectified, roll_by, -1) for roll_by in (1, 2, 3)], -1)

def path_masks(parent_row):
    places = jnp.arange(SEGS, dtype=jnp.int32)
    base_index = places // TREE * TREE
    members = base_index[:, None] + jnp.arange(TREE, dtype=jnp.int32)[None, :]
    current = parent_row.astype(jnp.int32)
    ancestors = jnp.zeros((SEGS, TREE), jnp.float32)
    for hop_index in range(TREE - 1):
        ancestors = ancestors + (members == current[:, None]).astype(jnp.float32)
        looked = lax.optimization_barrier(jnp.sum(jnp.where(current[:, None] == places[None, :], parent_row[None, :], 0), axis=1)).astype(jnp.int32)
        current = jnp.where(current >= 0, looked, -1).astype(jnp.int32)
    return jnp.repeat(ancestors, MEM, axis=1).reshape(SEGS // TREE, TREE, TREE * MEM)

def group_block(segment_rows, path_mask, key_feats, mem_values, weights):
    qkv_weight, head_bias, out_weight, up_weight, up_bias, down_weight, mem_qk, mem_value, norm_gain, shift_bias = weights
    query = low_back(jnp.einsum('tsd,de->tse', segment_rows, mem_qk[0], precision=HIGHEST))
    query_feats = low(dpfp_features(query))
    assoc = low_back(jnp.einsum('tsf,rf->tsr', query_feats, key_feats, precision=HIGHEST)) * path_mask[:, None, :]
    read_weights = low(assoc)
    denominator = lax.optimization_barrier(jnp.sum(assoc, -1, keepdims=True)) + 1.0
    numerator = low_back(jnp.einsum('tsr,rd->tsd', read_weights, mem_values, precision=HIGHEST))
    hidden = segment_rows + numerator / denominator
    attn_in = low(layer_norm(hidden, norm_gain[0], shift_bias[0]))
    projected = jnp.einsum('tsd,dcf->tscf', attn_in, qkv_weight, precision=HIGHEST)
    bias_pair = head_bias.reshape(2, D)
    shape_heads = (TREE, SEG, HEADS, HEAD_DIM)
    queries = low(low_back(projected[:, :, 0] + bias_pair[0])).reshape(shape_heads)
    key_heads = low(low_back(projected[:, :, 1])).reshape(shape_heads)
    value_heads = low(low_back(projected[:, :, 2] + bias_pair[1])).reshape(shape_heads)
    scores = low_back(jnp.einsum('tqhd,tkhd->thqk', queries, key_heads, precision=HIGHEST) * HEAD_DIM ** (-0.5))
    positions = jnp.arange(SEG)
    causal = positions[:, None] >= positions[None, :]
    probs = jax.nn.softmax(jnp.where(causal, scores, -jnp.inf), axis=-1)
    attended = low(low_back(jnp.einsum('thqk,tkhd->tqhd', low(probs), value_heads, precision=HIGHEST))).reshape(TREE, SEG, D)
    attn_out = low_back(jnp.einsum('tsf,fd->tsd', attended, out_weight, precision=HIGHEST)) + shift_bias[2]
    middle = hidden + attn_out
    mlp_in = low(layer_norm(middle, norm_gain[1], shift_bias[1]))
    pre_act = low_back(jnp.einsum('tsd,df->tsf', mlp_in, up_weight, precision=HIGHEST) + up_bias.reshape(FF))
    activated = low(gelu_tanh(pre_act))
    return middle + jnp.einsum('tsf,fd->tsd', activated, down_weight, precision=HIGHEST) + shift_bias[3]

def forward(tokens_float, weights, parents):
    mem_qk = weights[6]
    mem_value = weights[7]
    groups = SEGS // TREE
    checked_block = jax.checkpoint(group_block)
    results = []
    for micro_index in range(MICRO):
        segment_rows = tokens_float[micro_index].reshape(SEGS, SEG, D)
        memory_rows = segment_rows[:, SEG - MEM:, :]
        mem_keys = low(low_back(jnp.einsum('nmd,de->nme', memory_rows, mem_qk[1], precision=HIGHEST)))
        mem_values = low(low_back(jnp.einsum('nmd,de->nme', memory_rows, mem_value, precision=HIGHEST)))
        key_feats = low(dpfp_features(mem_keys)).reshape(groups, TREE * MEM, 6 * D)
        value_rows = mem_values.reshape(groups, TREE * MEM, D)
        path_mask_all = path_masks(parents[micro_index])
        grouped = segment_rows.reshape(groups, TREE, SEG, D)
        outcome = lax.map(lambda group_item: checked_block(group_item[0], group_item[1], group_item[2], group_item[3], weights), (grouped, path_mask_all, key_feats, value_rows))
        results.append(outcome.reshape(TOKENS, D))
    return jnp.stack(results)

def reference(tokens, cotangent, qkv_weight, head_bias, out_weight, up_weight, up_bias, down_weight, mem_qk, mem_value, norm_gain, shift_bias, parents):
    weights = (qkv_weight.astype(jnp.float32), head_bias.astype(jnp.float32), out_weight.astype(jnp.float32), up_weight.astype(jnp.float32), up_bias.astype(jnp.float32), down_weight.astype(jnp.float32), mem_qk.astype(jnp.float32), mem_value.astype(jnp.float32), norm_gain.astype(jnp.float32), shift_bias.astype(jnp.float32))
    tokens_float = tokens.astype(jnp.float32)
    result, pullback = jax.vjp(lambda inputs, params: forward(inputs, params, parents), tokens_float, weights)
    grad_tokens, grad_weights = pullback(cotangent.astype(jnp.float32))
    return (result.astype(jnp.bfloat16), grad_tokens.astype(jnp.bfloat16), grad_weights[0], grad_weights[1], grad_weights[2], grad_weights[3], grad_weights[4], grad_weights[5], grad_weights[6], grad_weights[7], grad_weights[8], grad_weights[9])
```

```python
import jax
import jax.numpy as jnp
from jax import lax
from jax.experimental import pallas as pl
from jax.experimental.pallas import tpu as pltpu
from jax.sharding import PartitionSpec as P

HEAD_DIM = 64
MEM = 16
TREE = 8
MICRO = 2


EPSILON = 1e-05


def shifted(value, axis, steps):
    count = lax.axis_size(axis)
    initial, last = (max(0, -steps), min(count, count - steps))
    return lax.ppermute(value, axis, [(source, source + steps) for source in range(initial, last)])


def layer_norm(values, gains, offset):
    center = values - jnp.mean(values, -1, keepdims=True)
    spread = jnp.mean(center * center, -1, keepdims=True)
    return center * lax.rsqrt(spread + EPSILON) * gains + offset


def gelu_tanh(values):
    return jax.nn.gelu(values, approximate=True)


def rectify(values):
    return jnp.concatenate([jax.nn.relu(values), jax.nn.relu(-values)], -1)


def dpfp_rounded(values):
    rectified = rectify(values)
    return jnp.concatenate(
        [
            (rectified * jnp.roll(rectified, roll_by, -1)).astype(jnp.bfloat16)
            for roll_by in (1, 2, 3)
        ],
        -1,
    )


def dpfp_backward(values, grad_feats):
    rectified = rectify(values)
    width = rectified.shape[1]
    grad_rect = jnp.zeros_like(rectified)
    for place, roll_by in enumerate((1, 2, 3)):
        piece = grad_feats[:, place * width : (place + 1) * width]
        grad_rect = (
            grad_rect
            + piece * jnp.roll(rectified, roll_by, -1)
            + jnp.roll(piece * rectified, -roll_by, -1)
        )
    half = width // 2
    positive = (values > 0).astype(jnp.float32)
    negative = (values < 0).astype(jnp.float32)
    return grad_rect[:, :half] * positive - grad_rect[:, half:] * negative


def divide_rows(top_part, bottom_part):
    return top_part / bottom_part


def inner_rows(left, right):
    return lax.dot_general(
        left, right, (((0,), (0,)), ((), ())), preferred_element_type=jnp.float32
    )


def outer_cols(left, right):
    return lax.dot_general(
        left, right, (((1,), (1,)), ((), ())), preferred_element_type=jnp.float32
    )


def path_marks(parent_row, own_index):
    seg_count = parent_row.shape[0]
    places = jnp.arange(seg_count, dtype=jnp.int32)

    def parent_of(position):
        return jnp.sum(jnp.where(places == position, parent_row, 0))

    current = parent_of(own_index)
    base_index = own_index // TREE * TREE
    members = base_index + jnp.arange(TREE, dtype=jnp.int32)
    ancestors = jnp.zeros((TREE,), jnp.float32)
    for hop_index in range(TREE - 1):
        ancestors = ancestors + (members == current).astype(jnp.float32)
        current = jnp.where(current >= 0, parent_of(current), -1)
    return ancestors


def generic_body(
    tokens,
    cotangent,
    qkv_weight,
    head_bias,
    out_weight,
    up_weight,
    up_bias,
    down_weight,
    mem_qk,
    mem_value,
    norm_gain,
    shift_bias,
    parents,
):
    own_index = lax.axis_index("dp")
    own_slot = own_index % TREE
    seg_len = tokens.shape[1]
    model_width = mem_value.shape[1]
    local_cols = qkv_weight.shape[2]
    heads_local = local_cols // HEAD_DIM
    group_rows = TREE * MEM
    score_scale = HEAD_DIM ** (-0.5)
    share_rows = seg_len // lax.axis_size("mp")
    share_start = lax.axis_index("mp") * share_rows
    rows_index = jnp.arange(seg_len)
    causal = rows_index[:, None] >= rows_index[None, :]
    totals = None
    outputs = []
    input_grads = []
    for micro_index in range(MICRO):
        gathered = (
            lax.all_gather(qkv_weight, "dp", axis=0, tiled=True),
            lax.all_gather(head_bias, "dp", axis=2, tiled=True),
            lax.all_gather(out_weight, "dp", axis=1, tiled=True),
            lax.all_gather(up_weight, "dp", axis=0, tiled=True),
            lax.all_gather(up_bias, "dp", axis=1, tiled=True),
            lax.all_gather(down_weight, "dp", axis=1, tiled=True),
            lax.all_gather(mem_qk, "dp", axis=1, tiled=True),
            lax.all_gather(mem_value, "dp", axis=0, tiled=True),
            lax.all_gather(norm_gain, "dp", axis=1, tiled=True),
            lax.all_gather(shift_bias, "dp", axis=1, tiled=True),
        )
        (
            qkv_full,
            hbias_full,
            outw_full,
            upw_full,
            ubias_full,
            downw_full,
            memqk_full,
            memv_full,
            gains_full,
            shifts_full,
        ) = gathered
        inputs = tokens[micro_index]
        memory_rows = inputs[seg_len - MEM :]
        key_raw = jnp.dot(memory_rows, memqk_full[1], preferred_element_type=jnp.float32)
        value_raw = jnp.dot(memory_rows, memv_full, preferred_element_type=jnp.float32)
        key_low = key_raw.astype(jnp.bfloat16)
        value_low = value_raw.astype(jnp.bfloat16)
        empty_group = jnp.zeros((group_rows, model_width), jnp.bfloat16)
        group_keys = lax.dynamic_update_slice_in_dim(empty_group, key_low, own_slot * MEM, 0)
        group_values = lax.dynamic_update_slice_in_dim(empty_group, value_low, own_slot * MEM, 0)
        for hop_count in range(1, TREE):
            far_keys, far_values = shifted((key_low, value_low), "dp", hop_count)
            far_slot = own_slot - hop_count
            inside = far_slot >= 0
            place_at = jnp.maximum(far_slot, 0) * MEM
            group_keys = jnp.where(
                inside,
                lax.dynamic_update_slice_in_dim(group_keys, far_keys, place_at, 0),
                group_keys,
            )
            group_values = jnp.where(
                inside,
                lax.dynamic_update_slice_in_dim(group_values, far_values, place_at, 0),
                group_values,
            )
        group_keys_f = group_keys.astype(jnp.float32)
        key_feats = dpfp_rounded(group_keys_f)
        row_mask = jnp.repeat(path_marks(parents[micro_index], own_index), MEM)
        query_raw = jnp.dot(inputs, memqk_full[0], preferred_element_type=jnp.float32)
        query_feats = dpfp_rounded(query_raw)
        masked_scores = outer_cols(query_feats, key_feats) * row_mask[None, :]
        read_weights = masked_scores.astype(jnp.bfloat16)
        denominator = jnp.sum(masked_scores, -1, keepdims=True) + 1.0
        numerator = jnp.dot(read_weights, group_values, preferred_element_type=jnp.float32)
        hidden = inputs.astype(jnp.float32) + numerator / denominator
        attn_in = layer_norm(hidden, gains_full[0], shifts_full[0]).astype(jnp.bfloat16)
        projected = jnp.einsum("sd,dcf->scf", attn_in, qkv_full, preferred_element_type=jnp.float32)
        bias_pair = hbias_full.reshape(2, local_cols).astype(jnp.float32)
        shape_heads = (seg_len, heads_local, HEAD_DIM)
        queries = (projected[:, 0] + bias_pair[0]).astype(jnp.bfloat16).reshape(shape_heads)
        key_heads = projected[:, 1].astype(jnp.bfloat16).reshape(shape_heads)
        value_heads = (projected[:, 2] + bias_pair[1]).astype(jnp.bfloat16).reshape(shape_heads)
        scores = (
            jnp.einsum("qhd,khd->hqk", queries, key_heads, preferred_element_type=jnp.float32)
            * score_scale
        )
        scores = jnp.where(causal[None], scores, -jnp.inf)
        row_max = jnp.max(scores, -1, keepdims=True)
        exponents = jnp.exp(scores - row_max)
        row_total = jnp.sum(exponents, -1, keepdims=True)
        log_total = row_max + jnp.log(row_total)
        prob_low = (exponents / row_total).astype(jnp.bfloat16)
        attended = jnp.einsum(
            "hqk,khd->qhd", prob_low, value_heads, preferred_element_type=jnp.float32
        )
        attended = attended.astype(jnp.bfloat16).reshape(seg_len, local_cols)
        attn_out = (
            lax.psum(
                jnp.dot(attended, outw_full, preferred_element_type=jnp.float32).astype(
                    jnp.bfloat16
                ),
                "mp",
            ).astype(jnp.float32)
            + shifts_full[2]
        )
        middle = hidden + attn_out
        normed_two = layer_norm(middle, gains_full[1], shifts_full[1]).astype(jnp.bfloat16)
        pre_act = jnp.dot(normed_two, upw_full, preferred_element_type=jnp.float32) + ubias_full[0]
        activated = gelu_tanh(pre_act).astype(jnp.bfloat16)
        mlp_share = lax.psum_scatter(
            jnp.dot(activated, downw_full, preferred_element_type=jnp.float32).astype(jnp.bfloat16),
            "mp",
            scatter_dimension=0,
            tiled=True,
        ).astype(jnp.float32)
        middle_share = lax.dynamic_slice_in_dim(middle, share_start, share_rows, 0)
        outputs.append((middle_share + mlp_share + shifts_full[3]).astype(jnp.bfloat16))
        weights_again = (
            lax.all_gather(qkv_weight, "dp", axis=0, tiled=True),
            lax.all_gather(head_bias, "dp", axis=2, tiled=True),
            lax.all_gather(out_weight, "dp", axis=1, tiled=True),
            lax.all_gather(up_weight, "dp", axis=0, tiled=True),
            lax.all_gather(up_bias, "dp", axis=1, tiled=True),
            lax.all_gather(down_weight, "dp", axis=1, tiled=True),
            lax.all_gather(mem_qk, "dp", axis=1, tiled=True),
            lax.all_gather(mem_value, "dp", axis=0, tiled=True),
            lax.all_gather(norm_gain, "dp", axis=1, tiled=True),
            lax.all_gather(shift_bias, "dp", axis=1, tiled=True),
        )
        qkv_back = weights_again[0]
        outw_back = weights_again[2]
        upw_back = weights_again[3]
        downw_back = weights_again[5]
        memqk_back = weights_again[6]
        memv_back = weights_again[7]
        gains_back = weights_again[8]
        shifts_back = weights_again[9]
        grad_out = cotangent[micro_index]
        grad_out_f = grad_out.astype(jnp.float32)
        grad_downw = inner_rows(activated, grad_out)
        grad_act = outer_cols(grad_out, downw_back)
        gelu_value, gelu_back = jax.vjp(gelu_tanh, pre_act)
        grad_pre = gelu_back(grad_act)[0].astype(jnp.bfloat16)
        grad_ubias = jnp.sum(grad_pre.astype(jnp.float32), 0)[None, :]
        grad_upw = inner_rows(normed_two, grad_pre)
        grad_norm_two = lax.psum(outer_cols(grad_pre, upw_back).astype(jnp.bfloat16), "mp").astype(
            jnp.float32
        )
        norm_value, norm_two_back = jax.vjp(layer_norm, middle, gains_back[1], shifts_back[1])
        grad_mid_norm, gain_two, shift_two = norm_two_back(grad_norm_two)
        grad_middle = grad_out_f + grad_mid_norm
        grad_attn = grad_middle.astype(jnp.bfloat16)
        grad_outw = inner_rows(attended, grad_attn)
        grad_attended = outer_cols(grad_attn, outw_back).astype(jnp.bfloat16).reshape(shape_heads)
        scores_again = (
            jnp.einsum("qhd,khd->hqk", queries, key_heads, preferred_element_type=jnp.float32)
            * score_scale
        )
        scores_again = jnp.where(causal[None], scores_again, -jnp.inf)
        prob_full = jnp.exp(scores_again - log_total)
        prob_again = prob_full.astype(jnp.bfloat16)
        grad_values = jnp.einsum(
            "hqk,qhd->khd", prob_again, grad_attended, preferred_element_type=jnp.float32
        )
        grad_probs = jnp.einsum(
            "qhd,khd->hqk", grad_attended, value_heads, preferred_element_type=jnp.float32
        )
        row_delta = jnp.sum(prob_full * grad_probs, -1, keepdims=True)
        grad_scores = (prob_full * (grad_probs - row_delta)).astype(jnp.bfloat16)
        grad_queries = (
            jnp.einsum("hqk,khd->qhd", grad_scores, key_heads, preferred_element_type=jnp.float32)
            * score_scale
        )
        grad_keys = (
            jnp.einsum("hqk,qhd->khd", grad_scores, queries, preferred_element_type=jnp.float32)
            * score_scale
        )
        grad_proj = (
            jnp.stack([grad_queries, grad_keys, grad_values], 1)
            .reshape(seg_len, 3, local_cols)
            .astype(jnp.bfloat16)
        )
        grad_proj_f = grad_proj.astype(jnp.float32)
        grad_hbias = jnp.stack(
            [jnp.sum(grad_proj_f[:, 0], 0), jnp.sum(grad_proj_f[:, 2], 0)]
        ).reshape(2, 1, local_cols)
        grad_qkv = jnp.einsum("sd,scf->dcf", attn_in, grad_proj, preferred_element_type=jnp.float32)
        grad_norm_one = lax.psum(
            jnp.einsum(
                "scf,dcf->sd", grad_proj, qkv_back, preferred_element_type=jnp.float32
            ).astype(jnp.bfloat16),
            "mp",
        ).astype(jnp.float32)
        norm_value_one, norm_one_back = jax.vjp(layer_norm, hidden, gains_back[0], shifts_back[0])
        grad_hid_norm, gain_one, shift_one = norm_one_back(grad_norm_one)
        grad_hidden = grad_middle + grad_hid_norm
        ratio_value, divide_back = jax.vjp(divide_rows, numerator, denominator)
        grad_numerator, grad_denominator = divide_back(grad_hidden)
        grad_numerator_b = grad_numerator.astype(jnp.bfloat16)
        grad_read = outer_cols(grad_numerator_b, group_values)
        grad_values_group = inner_rows(read_weights, grad_numerator_b)
        grad_assoc = ((grad_read + grad_denominator) * row_mask[None, :]).astype(jnp.bfloat16)
        grad_query_feats = jnp.dot(grad_assoc, key_feats, preferred_element_type=jnp.float32)
        grad_key_feats = inner_rows(grad_assoc, query_feats)
        grad_query = dpfp_backward(query_raw, grad_query_feats).astype(jnp.bfloat16)
        grad_keys_group = dpfp_backward(group_keys_f, grad_key_feats)
        own_keys = lax.dynamic_slice_in_dim(grad_keys_group, own_slot * MEM, MEM, 0)
        own_values = lax.dynamic_slice_in_dim(grad_values_group, own_slot * MEM, MEM, 0)
        for hop_count in range(1, TREE):
            far_slot = own_slot - hop_count
            inside = far_slot >= 0
            take_at = jnp.maximum(far_slot, 0) * MEM
            send_keys = jnp.where(
                inside, lax.dynamic_slice_in_dim(grad_keys_group, take_at, MEM, 0), 0.0
            )
            send_values = jnp.where(
                inside, lax.dynamic_slice_in_dim(grad_values_group, take_at, MEM, 0), 0.0
            )
            back_keys, back_values = (
                shifted(send_keys.astype(jnp.bfloat16), "dp", -hop_count).astype(send_keys.dtype),
                shifted(send_values.astype(jnp.bfloat16), "dp", -hop_count).astype(
                    send_values.dtype
                ),
            )
            arrive = own_slot + hop_count < TREE
            own_keys = own_keys + jnp.where(arrive, back_keys, 0.0)
            own_values = own_values + jnp.where(arrive, back_values, 0.0)
        own_keys_b = own_keys.astype(jnp.bfloat16)
        own_values_b = own_values.astype(jnp.bfloat16)
        grad_memqk = jnp.stack(
            [inner_rows(inputs, grad_query), inner_rows(memory_rows, own_keys_b)]
        )
        grad_memv = inner_rows(memory_rows, own_values_b)
        memory_part = outer_cols(own_keys_b, memqk_back[1]) + outer_cols(own_values_b, memv_back)
        padding = jnp.zeros((seg_len - MEM, model_width), jnp.float32)
        grad_inputs = (
            grad_hidden
            + outer_cols(grad_query, memqk_back[0])
            + jnp.concatenate([padding, memory_part], 0)
        )
        input_grads.append(grad_inputs.astype(jnp.bfloat16))
        grad_gains = jnp.stack([gain_one, gain_two])
        grad_shifts = jnp.stack(
            [shift_one, shift_two, jnp.sum(grad_middle, 0), jnp.sum(grad_out_f, 0)]
        )
        shares = (
            grad_qkv,
            grad_hbias,
            grad_outw,
            grad_upw,
            grad_ubias,
            grad_downw,
            grad_memqk,
            grad_memv,
            grad_gains,
            grad_shifts,
        )
        totals = (
            shares
            if totals is None
            else tuple((older + newer for older, newer in zip(totals, shares)))
        )
    (
        sum_qkv,
        sum_hbias,
        sum_outw,
        sum_upw,
        sum_ubias,
        sum_downw,
        sum_memqk,
        sum_memv,
        sum_gains,
        sum_shifts,
    ) = totals
    totals = (
        lax.psum_scatter(sum_qkv, "dp", scatter_dimension=0, tiled=True),
        lax.psum_scatter(sum_hbias, "dp", scatter_dimension=2, tiled=True),
        lax.psum_scatter(sum_outw, "dp", scatter_dimension=1, tiled=True),
        lax.psum_scatter(sum_upw, "dp", scatter_dimension=0, tiled=True),
        lax.psum_scatter(sum_ubias, "dp", scatter_dimension=1, tiled=True),
        lax.psum_scatter(sum_downw, "dp", scatter_dimension=1, tiled=True),
        lax.psum_scatter(sum_memqk, "dp", scatter_dimension=1, tiled=True),
        lax.psum_scatter(sum_memv, "dp", scatter_dimension=0, tiled=True),
        lax.psum_scatter(sum_gains.astype(jnp.float32), "dp", scatter_dimension=1, tiled=True),
        lax.psum_scatter(sum_shifts, "dp", scatter_dimension=1, tiled=True),
    )
    mixed = jnp.stack(outputs)
    tokens_grad = jnp.stack(input_grads)
    return (mixed, tokens_grad) + tuple(totals)


RING = 8
BF = jnp.bfloat16
F32 = jnp.float32


def ring_dp(place):
    high = place // 4
    return high * (2 * (7 - place) + 1) + (1 - high) * (2 * place)


def ring_place(index):
    y_at = index % 2
    z_at = index // 2
    return y_at * (7 - z_at) + (1 - y_at) * z_at


def ring_at(place, steps):
    return ring_dp((place + steps + 2 * RING) % RING)


def ring_barrier(right, left):
    barrier = pltpu.get_barrier_semaphore()
    for other in (right, left):
        pl.semaphore_signal(
            barrier, inc=1, device_id={"dp": other}, device_id_type=pl.DeviceIdType.MESH
        )
    pl.semaphore_wait(barrier, 2)


def half_rows(ref, direction):
    half = ref.shape[-2] // 2
    return ref.at[pl.ds(direction * half, half)]


def gather_kernel(count, *refs):
    ins, outs = refs[:count], refs[count : 2 * count]
    send_sem, recv_sem, own_sem = refs[2 * count :]
    own = lax.axis_index("dp")
    place = ring_place(own)
    sides = (ring_at(place, 1), ring_at(place, -1))
    ring_barrier(*sides)

    def copy(at, direction, step):
        origin = ring_at(place, (1 - step) * (1 - 2 * direction))
        source = ins[at] if step == 1 else outs[at].at[origin]
        target = outs[at].at[origin]
        if step == 4:
            source, target = half_rows(source, direction), half_rows(target, direction)
        return pltpu.make_async_remote_copy(
            src_ref=source,
            dst_ref=target,
            send_sem=send_sem.at[at, direction, step - 1],
            recv_sem=recv_sem.at[at, direction, step - 1],
            device_id={"dp": sides[direction]},
            device_id_type=pl.DeviceIdType.MESH,
        )

    mine = [
        pltpu.make_async_copy(ins[at], outs[at].at[own], own_sem.at[at]) for at in range(count)
    ]
    for at in range(count):
        for direction in (0, 1):
            copy(at, direction, 1).start()
        mine[at].start()
    for step in range(2, 5):
        for at in range(count):
            for direction in (0, 1):
                copy(at, direction, step - 1).wait_recv()
                copy(at, direction, step).start()
    for at in range(count):
        for direction in (0, 1):
            copy(at, direction, 4).wait_recv()
        mine[at].wait()
    for at in range(count):
        for direction in (0, 1):
            for step in range(1, 5):
                copy(at, direction, step).wait_send()


def ring_gather(*arrays):
    count = len(arrays)
    return pl.pallas_call(
        lambda *refs: gather_kernel(count, *refs),
        out_shape=[jax.ShapeDtypeStruct((RING,) + a.shape, a.dtype) for a in arrays],
        in_specs=[pl.BlockSpec(memory_space=pltpu.VMEM)] * count,
        out_specs=[pl.BlockSpec(memory_space=pltpu.VMEM)] * count,
        scratch_shapes=[
            pltpu.SemaphoreType.DMA((count, 2, 4)),
            pltpu.SemaphoreType.DMA((count, 2, 4)),
            pltpu.SemaphoreType.DMA((count,)),
        ],
        compiler_params=pltpu.CompilerParams(collective_id=0, has_side_effects=True),
        name="ring_gather",
    )(*arrays)


def scatter_kernel(count, *refs):
    ins, outs = refs[:count], refs[count : 2 * count]
    bufs = refs[2 * count : 3 * count]
    send_sem, recv_sem = refs[3 * count :]
    own = lax.axis_index("dp")
    place = ring_place(own)
    sides = (ring_at(place, 1), ring_at(place, -1))
    ring_barrier(*sides)

    def copy(at, direction, step):
        source = bufs[at].at[direction, step - 1]
        target = bufs[at].at[direction, step]
        if step == 1:
            source, target = half_rows(source, direction), half_rows(target, direction)
        return pltpu.make_async_remote_copy(
            src_ref=source,
            dst_ref=target,
            send_sem=send_sem.at[at, direction, step - 1],
            recv_sem=recv_sem.at[at, direction, step - 1],
            device_id={"dp": sides[direction]},
            device_id_type=pl.DeviceIdType.MESH,
        )

    def term(at, direction, step):
        aim = ring_at(place, (5 - step) * (1 - 2 * direction))
        return ins[at].at[aim]

    for at in range(count):
        for direction in (0, 1):
            half = outs[at].shape[0] // 2
            part = pl.ds(direction * half, half)
            bufs[at][direction, 0, part] = term(at, direction, 1)[part].astype(bufs[at].dtype)
            copy(at, direction, 1).start()
    for step in range(2, 5):
        for at in range(count):
            for direction in (0, 1):
                buf = bufs[at]
                copy(at, direction, step - 1).wait_recv()
                if step == 2:
                    half = outs[at].shape[0] // 2
                    part = pl.ds(direction * half, half)
                    rest = pl.ds((1 - direction) * half, half)
                    buf[direction, 1, part] = (
                        buf[direction, 1, part].astype(F32) + term(at, direction, 2)[part]
                    ).astype(buf.dtype)
                    buf[direction, 1, rest] = term(at, direction, 2)[rest].astype(buf.dtype)
                else:
                    buf[direction, step - 1] = (
                        buf[direction, step - 1].astype(F32) + term(at, direction, step)[...]
                    ).astype(buf.dtype)
                copy(at, direction, step).start()
    for at in range(count):
        for direction in (0, 1):
            copy(at, direction, 4).wait_recv()
        outs[at][...] = (
            ins[at][own] + bufs[at][0, 4].astype(F32) + bufs[at][1, 4].astype(F32)
        )
    for at in range(count):
        for direction in (0, 1):
            for step in range(1, 5):
                copy(at, direction, step).wait_send()


def ring_scatter(arrays, kinds):
    count = len(arrays)
    return pl.pallas_call(
        lambda *refs: scatter_kernel(count, *refs),
        out_shape=[jax.ShapeDtypeStruct(a.shape[1:], F32) for a in arrays],
        in_specs=[pl.BlockSpec(memory_space=pltpu.VMEM)] * count,
        out_specs=[pl.BlockSpec(memory_space=pltpu.VMEM)] * count,
        scratch_shapes=[
            pltpu.VMEM((2, 5) + a.shape[1:], kind) for a, kind in zip(arrays, kinds)
        ]
        + [pltpu.SemaphoreType.DMA((count, 2, 4)), pltpu.SemaphoreType.DMA((count, 2, 4))],
        compiler_params=pltpu.CompilerParams(
            collective_id=1, has_side_effects=True, vmem_limit_bytes=60 * 1024 * 1024
        ),
        name="ring_scatter",
    )(*arrays)


def gather_weights(
    qkv_weight, head_bias, out_weight, up_weight, up_bias, down_weight, mem_qk, mem_value,
    norm_gain, shift_bias,
):
    rows, parts, cols = qkv_weight.shape
    small = jnp.concatenate(
        [
            jnp.pad(head_bias[:, 0], ((0, 0), (0, rows - head_bias.shape[2]))),
            up_bias,
            norm_gain,
            shift_bias,
        ],
        0,
    )
    small = jnp.pad(small, ((0, 32 - small.shape[0]), (0, 128 - rows)))
    memk, memv, memq, qkv, outw, upw, downw, small = ring_gather(
        mem_qk[1], mem_value, mem_qk[0], qkv_weight.reshape(rows, parts * cols), out_weight.T,
        up_weight, down_weight.T, small,
    )
    width = RING * rows
    rows_of = small[:, :9, :rows].transpose(1, 0, 2)
    flat = rows_of.reshape(9, width)
    hbias = rows_of[:2, :, : head_bias.shape[2]].reshape(2, 1, -1)
    return (
        qkv.reshape(width, parts, cols),
        hbias,
        outw.reshape(width, -1).T,
        upw.reshape(width, -1),
        flat[2:3],
        downw.reshape(width, -1).T,
        jnp.stack([memq.reshape(width, width), memk.reshape(width, width)]),
        memv.reshape(width, width),
        flat[3:5],
        flat[5:9],
    )


def scatter_grads(qkv, hbias, outw, upw, ubias, downw, memqk, memv, gains, shifts):
    width, parts, cols = qkv.shape
    rows = width // RING
    heads = cols // RING
    small = jnp.concatenate(
        [
            jnp.pad(hbias.reshape(2, RING, heads), ((0, 0), (0, 0), (0, rows - heads))),
            ubias.reshape(1, RING, rows),
            gains.reshape(2, RING, rows),
            shifts.reshape(4, RING, rows),
        ],
        0,
    ).transpose(1, 0, 2)
    small = jnp.pad(small, ((0, 0), (0, 16 - 9), (0, 128 - rows)))

    def cut(value):
        return value.reshape(RING, rows, -1)

    down, up, out, qkv, memq, memk, memv, small = ring_scatter(
        [
            cut(downw.T), cut(upw), cut(outw.T), cut(qkv.reshape(width, -1)), cut(memqk[0]),
            cut(memqk[1]), cut(memv), small,
        ],
        [BF] * 7 + [F32],
    )
    return (
        qkv.reshape(rows, parts, cols),
        small[:2, :heads].reshape(2, 1, heads),
        out.T,
        up,
        small[2:3, :rows],
        down.T,
        jnp.stack([memq, memk]),
        memv,
        small[3:5, :rows],
        small[5:9, :rows],
    )


def ring_body(
    tokens,
    cotangent,
    qkv_weight,
    head_bias,
    out_weight,
    up_weight,
    up_bias,
    down_weight,
    mem_qk,
    mem_value,
    norm_gain,
    shift_bias,
    parents,
):
    own_index = lax.axis_index("dp")
    own_slot = own_index % TREE
    seg_len = tokens.shape[1]
    model_width = mem_value.shape[1]
    local_cols = qkv_weight.shape[2]
    heads_local = local_cols // HEAD_DIM
    group_rows = TREE * MEM
    score_scale = HEAD_DIM ** (-0.5)
    share_rows = seg_len // lax.axis_size("mp")
    share_start = lax.axis_index("mp") * share_rows
    rows_index = jnp.arange(seg_len)
    causal = rows_index[:, None] >= rows_index[None, :]
    totals = None
    (qkv_full, hbias_full, outw_full, upw_full, ubias_full, downw_full, memqk_full, memv_full,
     gains_full, shifts_full) = gather_weights(
        qkv_weight, head_bias, out_weight, up_weight, up_bias, down_weight, mem_qk, mem_value,
        norm_gain, shift_bias)
    outputs = []
    input_grads = []
    for micro_index in range(MICRO):
        inputs = tokens[micro_index]
        memory_rows = inputs[seg_len - MEM :]
        key_raw = jnp.dot(memory_rows, memqk_full[1], preferred_element_type=jnp.float32)
        value_raw = jnp.dot(memory_rows, memv_full, preferred_element_type=jnp.float32)
        key_low = key_raw.astype(jnp.bfloat16)
        value_low = value_raw.astype(jnp.bfloat16)
        empty_group = jnp.zeros((group_rows, model_width), jnp.bfloat16)
        group_keys = lax.dynamic_update_slice_in_dim(empty_group, key_low, own_slot * MEM, 0)
        group_values = lax.dynamic_update_slice_in_dim(empty_group, value_low, own_slot * MEM, 0)
        for hop_count in range(1, TREE):
            far_keys, far_values = shifted((key_low, value_low), "dp", hop_count)
            far_slot = own_slot - hop_count
            inside = far_slot >= 0
            place_at = jnp.maximum(far_slot, 0) * MEM
            group_keys = jnp.where(
                inside,
                lax.dynamic_update_slice_in_dim(group_keys, far_keys, place_at, 0),
                group_keys,
            )
            group_values = jnp.where(
                inside,
                lax.dynamic_update_slice_in_dim(group_values, far_values, place_at, 0),
                group_values,
            )
        group_keys_f = group_keys.astype(jnp.float32)
        key_feats = dpfp_rounded(group_keys_f)
        row_mask = jnp.repeat(path_marks(parents[micro_index], own_index), MEM)
        query_raw = jnp.dot(inputs, memqk_full[0], preferred_element_type=jnp.float32)
        query_feats = dpfp_rounded(query_raw)
        masked_scores = outer_cols(query_feats, key_feats) * row_mask[None, :]
        read_weights = masked_scores.astype(jnp.bfloat16)
        denominator = jnp.sum(masked_scores, -1, keepdims=True) + 1.0
        numerator = jnp.dot(read_weights, group_values, preferred_element_type=jnp.float32)
        hidden = inputs.astype(jnp.float32) + numerator / denominator
        attn_in = layer_norm(hidden, gains_full[0], shifts_full[0]).astype(jnp.bfloat16)
        projected = jnp.einsum("sd,dcf->scf", attn_in, qkv_full, preferred_element_type=jnp.float32)
        bias_pair = hbias_full.reshape(2, local_cols).astype(jnp.float32)
        shape_heads = (seg_len, heads_local, HEAD_DIM)
        queries = (projected[:, 0] + bias_pair[0]).astype(jnp.bfloat16).reshape(shape_heads)
        key_heads = projected[:, 1].astype(jnp.bfloat16).reshape(shape_heads)
        value_heads = (projected[:, 2] + bias_pair[1]).astype(jnp.bfloat16).reshape(shape_heads)
        scores = (
            jnp.einsum("qhd,khd->hqk", queries, key_heads, preferred_element_type=jnp.float32)
            * score_scale
        )
        scores = jnp.where(causal[None], scores, -jnp.inf)
        row_max = jnp.max(scores, -1, keepdims=True)
        exponents = jnp.exp(scores - row_max)
        row_total = jnp.sum(exponents, -1, keepdims=True)
        log_total = row_max + jnp.log(row_total)
        prob_low = (exponents / row_total).astype(jnp.bfloat16)
        attended = jnp.einsum(
            "hqk,khd->qhd", prob_low, value_heads, preferred_element_type=jnp.float32
        )
        attended = attended.astype(jnp.bfloat16).reshape(seg_len, local_cols)
        attn_out = (
            lax.psum(
                jnp.dot(attended, outw_full, preferred_element_type=jnp.float32).astype(
                    jnp.bfloat16
                ),
                "mp",
            ).astype(jnp.float32)
            + shifts_full[2]
        )
        middle = hidden + attn_out
        normed_two = layer_norm(middle, gains_full[1], shifts_full[1]).astype(jnp.bfloat16)
        pre_act = jnp.dot(normed_two, upw_full, preferred_element_type=jnp.float32) + ubias_full[0]
        activated = gelu_tanh(pre_act).astype(jnp.bfloat16)
        mlp_share = lax.psum_scatter(
            jnp.dot(activated, downw_full, preferred_element_type=jnp.float32).astype(jnp.bfloat16),
            "mp",
            scatter_dimension=0,
            tiled=True,
        ).astype(jnp.float32)
        middle_share = lax.dynamic_slice_in_dim(middle, share_start, share_rows, 0)
        outputs.append((middle_share + mlp_share + shifts_full[3]).astype(jnp.bfloat16))
        qkv_back, outw_back, upw_back, downw_back = qkv_full, outw_full, upw_full, downw_full
        memqk_back, memv_back, gains_back, shifts_back = memqk_full, memv_full, gains_full, shifts_full
        grad_out = cotangent[micro_index]
        grad_out_f = grad_out.astype(jnp.float32)
        grad_downw = inner_rows(activated, grad_out)
        grad_act = outer_cols(grad_out, downw_back)
        gelu_value, gelu_back = jax.vjp(gelu_tanh, pre_act)
        grad_pre = gelu_back(grad_act)[0].astype(jnp.bfloat16)
        grad_ubias = jnp.sum(grad_pre.astype(jnp.float32), 0)[None, :]
        grad_upw = inner_rows(normed_two, grad_pre)
        grad_norm_two = lax.psum(outer_cols(grad_pre, upw_back).astype(jnp.bfloat16), "mp").astype(
            jnp.float32
        )
        norm_value, norm_two_back = jax.vjp(layer_norm, middle, gains_back[1], shifts_back[1])
        grad_mid_norm, gain_two, shift_two = norm_two_back(grad_norm_two)
        grad_middle = grad_out_f + grad_mid_norm
        grad_attn = grad_middle.astype(jnp.bfloat16)
        grad_outw = inner_rows(attended, grad_attn)
        grad_attended = outer_cols(grad_attn, outw_back).astype(jnp.bfloat16).reshape(shape_heads)
        scores_again = (
            jnp.einsum("qhd,khd->hqk", queries, key_heads, preferred_element_type=jnp.float32)
            * score_scale
        )
        scores_again = jnp.where(causal[None], scores_again, -jnp.inf)
        prob_full = jnp.exp(scores_again - log_total)
        prob_again = prob_full.astype(jnp.bfloat16)
        grad_values = jnp.einsum(
            "hqk,qhd->khd", prob_again, grad_attended, preferred_element_type=jnp.float32
        )
        grad_probs = jnp.einsum(
            "qhd,khd->hqk", grad_attended, value_heads, preferred_element_type=jnp.float32
        )
        row_delta = jnp.sum(prob_full * grad_probs, -1, keepdims=True)
        grad_scores = (prob_full * (grad_probs - row_delta)).astype(jnp.bfloat16)
        grad_queries = (
            jnp.einsum("hqk,khd->qhd", grad_scores, key_heads, preferred_element_type=jnp.float32)
            * score_scale
        )
        grad_keys = (
            jnp.einsum("hqk,qhd->khd", grad_scores, queries, preferred_element_type=jnp.float32)
            * score_scale
        )
        grad_proj = (
            jnp.stack([grad_queries, grad_keys, grad_values], 1)
            .reshape(seg_len, 3, local_cols)
            .astype(jnp.bfloat16)
        )
        grad_proj_f = grad_proj.astype(jnp.float32)
        grad_hbias = jnp.stack(
            [jnp.sum(grad_proj_f[:, 0], 0), jnp.sum(grad_proj_f[:, 2], 0)]
        ).reshape(2, 1, local_cols)
        grad_qkv = jnp.einsum("sd,scf->dcf", attn_in, grad_proj, preferred_element_type=jnp.float32)
        grad_norm_one = lax.psum(
            jnp.einsum(
                "scf,dcf->sd", grad_proj, qkv_back, preferred_element_type=jnp.float32
            ).astype(jnp.bfloat16),
            "mp",
        ).astype(jnp.float32)
        norm_value_one, norm_one_back = jax.vjp(layer_norm, hidden, gains_back[0], shifts_back[0])
        grad_hid_norm, gain_one, shift_one = norm_one_back(grad_norm_one)
        grad_hidden = grad_middle + grad_hid_norm
        ratio_value, divide_back = jax.vjp(divide_rows, numerator, denominator)
        grad_numerator, grad_denominator = divide_back(grad_hidden)
        grad_numerator_b = grad_numerator.astype(jnp.bfloat16)
        grad_read = outer_cols(grad_numerator_b, group_values)
        grad_values_group = inner_rows(read_weights, grad_numerator_b)
        grad_assoc = ((grad_read + grad_denominator) * row_mask[None, :]).astype(jnp.bfloat16)
        grad_query_feats = jnp.dot(grad_assoc, key_feats, preferred_element_type=jnp.float32)
        grad_key_feats = inner_rows(grad_assoc, query_feats)
        grad_query = dpfp_backward(query_raw, grad_query_feats).astype(jnp.bfloat16)
        grad_keys_group = dpfp_backward(group_keys_f, grad_key_feats)
        own_keys = lax.dynamic_slice_in_dim(grad_keys_group, own_slot * MEM, MEM, 0)
        own_values = lax.dynamic_slice_in_dim(grad_values_group, own_slot * MEM, MEM, 0)
        for hop_count in range(1, TREE):
            far_slot = own_slot - hop_count
            inside = far_slot >= 0
            take_at = jnp.maximum(far_slot, 0) * MEM
            send_keys = jnp.where(
                inside, lax.dynamic_slice_in_dim(grad_keys_group, take_at, MEM, 0), 0.0
            )
            send_values = jnp.where(
                inside, lax.dynamic_slice_in_dim(grad_values_group, take_at, MEM, 0), 0.0
            )
            back_keys, back_values = (
                shifted(send_keys.astype(jnp.bfloat16), "dp", -hop_count).astype(send_keys.dtype),
                shifted(send_values.astype(jnp.bfloat16), "dp", -hop_count).astype(
                    send_values.dtype
                ),
            )
            arrive = own_slot + hop_count < TREE
            own_keys = own_keys + jnp.where(arrive, back_keys, 0.0)
            own_values = own_values + jnp.where(arrive, back_values, 0.0)
        own_keys_b = own_keys.astype(jnp.bfloat16)
        own_values_b = own_values.astype(jnp.bfloat16)
        grad_memqk = jnp.stack(
            [inner_rows(inputs, grad_query), inner_rows(memory_rows, own_keys_b)]
        )
        grad_memv = inner_rows(memory_rows, own_values_b)
        memory_part = outer_cols(own_keys_b, memqk_back[1]) + outer_cols(own_values_b, memv_back)
        padding = jnp.zeros((seg_len - MEM, model_width), jnp.float32)
        grad_inputs = (
            grad_hidden
            + outer_cols(grad_query, memqk_back[0])
            + jnp.concatenate([padding, memory_part], 0)
        )
        input_grads.append(grad_inputs.astype(jnp.bfloat16))
        grad_gains = jnp.stack([gain_one, gain_two])
        grad_shifts = jnp.stack(
            [shift_one, shift_two, jnp.sum(grad_middle, 0), jnp.sum(grad_out_f, 0)]
        )
        shares = (
            grad_qkv,
            grad_hbias,
            grad_outw,
            grad_upw,
            grad_ubias,
            grad_downw,
            grad_memqk,
            grad_memv,
            grad_gains,
            grad_shifts,
        )
        totals = (
            shares
            if totals is None
            else tuple((older + newer for older, newer in zip(totals, shares)))
        )
    (
        sum_qkv,
        sum_hbias,
        sum_outw,
        sum_upw,
        sum_ubias,
        sum_downw,
        sum_memqk,
        sum_memv,
        sum_gains,
        sum_shifts,
    ) = totals
    totals = scatter_grads(
        sum_qkv, sum_hbias, sum_outw, sum_upw, sum_ubias, sum_downw, sum_memqk, sum_memv,
        sum_gains, sum_shifts)
    mixed = jnp.stack(outputs)
    tokens_grad = jnp.stack(input_grads)
    return (mixed, tokens_grad) + tuple(totals)


def solution(mesh):
    body = ring_body if mesh.shape["dp"] == RING else generic_body
    return jax.shard_map(
        body,
        mesh=mesh,
        in_specs=(
            P(None, "dp", None),
            P(None, "dp", None),
            P("dp", None, "mp"),
            P(None, "mp", "dp"),
            P("mp", "dp"),
            P("dp", "mp"),
            P("mp", "dp"),
            P("mp", "dp"),
            P(None, "dp", None),
            P("dp", None),
            P(None, "dp"),
            P(None, "dp"),
            P(),
        ),
        out_specs=(
            P(None, ("dp", "mp"), None),
            P(None, "dp", None),
            P("dp", None, "mp"),
            P(None, "mp", "dp"),
            P("mp", "dp"),
            P("dp", "mp"),
            P("mp", "dp"),
            P("mp", "dp"),
            P(None, "dp", None),
            P("dp", None),
            P(None, "dp"),
            P(None, "dp"),
        ),
        check_vma=False,
    )
```
